256 devices in a mesh: solver: 128 (over z, y, x), ana: 2 (over core).
Axes of the slice: x: 4, y: 4, z: 8, core: 2. Of those that a mesh axis runs over, the one named last changes fastest.
Arguments:
- state: float32 [8192, 320], P(('solver', 'ana')), may hold values from -68 to 68
- history: bfloat16 [124, 8192, 320], P(None, ('solver', 'ana')), may hold values from -68 to 68
- inv_mass: float32 [64, 64, 8192], P(None, None, ('solver', 'ana')), may hold values from -1 to 3
- vol_op: float32 [320, 320], replicated, may hold values from -0.3125 to 0.3125
- lift_ops: float32 [6, 80, 320], replicated, may hold values from -0.625 to 0.625
- neighbors: int32 [6, 8192], P(None, ('solver', 'ana')), may hold values from -1 to 8191, as said below
- owner: int32 [8192], P(('solver', 'ana')), may hold values from 0 to 1, as said below
Outputs:
- coef: float32 [8192, 320, 128], P(('solver', 'ana'))
- factor: float32 [2, 128, 128], P('ana')
The draws below stay inside these ranges and needn't reach their ends.
Inputs may be any that keep to these rules, and one draw needn't show every extreme that they name: `neighbors`: the elements fill a grid of 2 x 8 x 512 cells along x (periodic), y (walls) and z (periodic); partition p = g * 2 + a holds the cells with y in a * 4 to (a + 1) * 4 - 1 and z in g * 4 to (g + 1) * 4 - 1 under the ids p * 32 to (p + 1) * 32 - 1 in some order; row f names the cell across face f, and -1 only across a wall. `owner`: every partition of 32 consecutive elements names every region exactly 16 times.
All inputs are finite; a program needn't handle non-finite values.
Results may differ from the reference program's by a relative error of at most 0.0003.
Values may be sent and summed in bfloat16 or wider, within the bound.
No kernel may reach another device: no remote copies, remote signals or barrier semaphores. Data moves between devices by JAX's collectives and lax.ppermute only.
A program may use at most 128 MiB of HBM per device.

```python
import math
import jax
import jax.numpy as jnp
import numpy as np
from jax import lax

FIELDS = 5
SIDE = 4
NODES = 64
C = 320
FC = 80
SNAPS = 128
STEPS = 4
HIST = 124
LX = 2
LY = 4
LZ = 4
E_DEV = 32
REGIONS = 2
GROUPS = 128
GY = 8
GZ = 512
ELEMS = 8192
PER_OWNER = 16
REGION_ROWS = 1310720


def draw_state(key, part):
    keys = jax.random.split(jax.random.fold_in(key, 11), 2)
    base = jnp.clip(jax.random.normal(keys[0], (ELEMS, C), jnp.float32), -4.0, 4.0)
    ramp = (1.0 + 2.0 * jnp.arange(ELEMS, dtype=jnp.float32) / (ELEMS - 1)) / 2.0
    column_scale = jnp.exp(jax.random.uniform(keys[1], (1, C), jnp.float32, math.log(0.3), math.log(3.0)))
    values = base * ramp[:, None] * column_scale
    return values.astype(jnp.float32)


def draw_history(key, part):
    keys = jax.random.split(jax.random.fold_in(key, 13), 2)
    base = jnp.clip(jax.random.normal(keys[0], (HIST, ELEMS, C), jnp.float32), -4.0, 4.0)
    ramp = (1.0 + 2.0 * jnp.arange(ELEMS, dtype=jnp.float32) / (ELEMS - 1)) / 2.0
    column_scale = jnp.exp(jax.random.uniform(keys[1], (1, 1, C), jnp.float32, math.log(0.3), math.log(3.0)))
    values = base * ramp[None, :, None] * column_scale
    return values.astype(jnp.bfloat16)


def draw_inv_mass(key, part):
    keys = jax.random.split(jax.random.fold_in(key, 17), 2)
    diagonal = jnp.exp(jax.random.uniform(keys[0], (1, 1, ELEMS), jnp.float32, math.log(0.5), math.log(2.0)))
    spread = jnp.clip(jax.random.normal(keys[1], (NODES, NODES, ELEMS), jnp.float32), -4.0, 4.0)
    spread = spread * (0.5 / math.sqrt(NODES))
    identity = jnp.eye(NODES, dtype=jnp.float32)[:, :, None]
    return (identity * diagonal + spread).astype(jnp.float32)


def draw_neighbors(key, part):
    partitions = GROUPS * REGIONS
    keys = jax.random.split(jax.random.fold_in(key, 23), partitions)
    perms = jax.vmap(lambda single: jax.random.permutation(single, E_DEV))(keys).astype(jnp.int32)
    labels = perms + (jnp.arange(partitions, dtype=jnp.int32) * E_DEV)[:, None]
    grid = labels.reshape(GROUPS, REGIONS, LZ, LY, LX)
    grid = jnp.transpose(grid, (0, 2, 1, 3, 4)).reshape(GZ, GY, LX)
    walls = jnp.full((GZ, 1, LX), -1, jnp.int32)
    across = [jnp.roll(grid, 1, axis=2), jnp.roll(grid, -1, axis=2), jnp.concatenate([walls, grid[:, :-1, :]], axis=1), jnp.concatenate([grid[:, 1:, :], walls], axis=1), jnp.roll(grid, 1, axis=0), jnp.roll(grid, -1, axis=0)]
    flat = grid.reshape(-1)
    result = jnp.zeros((6, ELEMS), jnp.int32)
    for face in range(6):
        result = result.at[face, flat].set(across[face].reshape(-1).astype(jnp.int32))
    return result


def draw_owner(key, part):
    partitions = GROUPS * REGIONS
    keys = jax.random.split(jax.random.fold_in(key, 29), partitions)
    pattern = (jnp.arange(E_DEV, dtype=jnp.int32) // PER_OWNER).astype(jnp.int32)
    shuffled = jax.vmap(lambda single: jax.random.permutation(single, pattern))(keys)
    return shuffled.reshape(-1).astype(jnp.int32)


def bell_draw(rng, dims, scale, bound, held_as=jnp.bfloat16):
    values = scale * jax.random.normal(rng, dims, jnp.float32)
    return jnp.clip(values, min=-bound, max=bound).astype(held_as)


def setup_inputs(seed: int = 0) -> dict:
    key_of = jax.random.split(jax.random.key(seed), 8)
    return {
        "state": draw_state(jax.random.fold_in(key_of[7], 71), 0),
        "history": draw_history(jax.random.fold_in(key_of[7], 71), 0),
        "inv_mass": draw_inv_mass(jax.random.fold_in(key_of[7], 71), 0),
        "vol_op": bell_draw(key_of[3], (C, C), C ** -0.5, 0.3125, jnp.float32),
        "lift_ops": bell_draw(key_of[4], (6, FC, C), FC ** -0.5, 0.625, jnp.float32),
        "neighbors": draw_neighbors(jax.random.fold_in(key_of[7], 71), 0),
        "owner": draw_owner(jax.random.fold_in(key_of[7], 71), 0),
    }


time_step = 0.2

def face_table(side):
    grid = np.arange(side ** 3).reshape(side, side, side)
    planes = [grid[:, :, 0], grid[:, :, side - 1], grid[:, 0, :], grid[:, side - 1, :], grid[0, :, :], grid[side - 1, :, :]]
    return np.stack([plane.reshape(-1) for plane in planes]).astype(np.int32)

def advance(field, neighbors, inv_mass, vol_op, lift_ops, table):
    highest = lax.Precision.HIGHEST
    count = field.shape[0]
    shaped = field.reshape(count, FIELDS, NODES)
    tendency = jnp.dot(field, vol_op, precision=highest)
    for face in range(6):
        contact = jnp.take(shaped, table[face ^ 1], axis=2).reshape(count, FC)
        target = neighbors[face]
        valid = target >= 0
        picked = jnp.take(contact, jnp.maximum(target, 0), axis=0)
        picked = jnp.where(valid[:, None], picked, jnp.zeros_like(picked))
        tendency = tendency + jnp.dot(picked, lift_ops[face], precision=highest)
    applied = jnp.einsum('efn,nme->efm', tendency.reshape(count, FIELDS, NODES), inv_mass, precision=highest)
    return field + time_step * applied.reshape(count, C)

def reference(state, history, inv_mass, vol_op, lift_ops, neighbors, owner):
    highest = lax.Precision.HIGHEST
    table = face_table(SIDE)
    field = state
    snapshots = []
    for step in range(STEPS):
        field = advance(field, neighbors, inv_mass, vol_op, lift_ops, table)
        snapshots.append(field)
    stacked = jnp.stack(snapshots)
    groups = owner.reshape(GROUPS, REGIONS * E_DEV)
    arranged = jnp.argsort(groups, axis=1, stable=True).astype(jnp.int32)
    offsets = jnp.arange(GROUPS, dtype=jnp.int32) * (REGIONS * E_DEV)
    arranged = (arranged + offsets[:, None]).astype(jnp.int32).reshape(GROUPS, REGIONS, E_DEV)

    def block_of(element_ids):
        earlier = jnp.take(history, element_ids, axis=1).astype(jnp.float32)
        latest = jnp.take(stacked, element_ids, axis=1)
        return jnp.concatenate([earlier, latest], axis=0).reshape(SNAPS, E_DEV * C)

    def group_gram(group_ids):

        def single_gram(element_ids):
            block = block_of(element_ids)
            return jnp.dot(block, block.T, precision=highest)
        return lax.map(single_gram, group_ids)
    gram = jnp.sum(lax.map(group_gram, arranged), axis=0) / REGION_ROWS
    lower = jnp.linalg.cholesky(gram)

    def group_coef(group_ids):

        def single_coef(member):
            element_ids, region_lower = member
            block = block_of(element_ids)
            solved = lax.linalg.triangular_solve(region_lower, block, left_side=True, lower=True)
            return solved.T.reshape(E_DEV, C, SNAPS)
        return lax.map(single_coef, (group_ids, lower))
    coef = lax.map(group_coef, arranged).reshape(ELEMS, C, SNAPS)
    return (coef, jnp.swapaxes(lower, 1, 2))
```

```python
import functools

import jax
import jax.numpy as jnp
from jax import lax
from jax.experimental import pallas as pl
from jax.experimental.pallas import tpu as pltpu
from jax.sharding import PartitionSpec as P

F32 = jnp.float32
BF16 = jnp.bfloat16
I32 = jnp.int32
HIGHEST = lax.Precision.HIGHEST

EL = 32
HALF = 16
C = 320
CP = 384
NODES = 64
HIST = 124
SNAPS = 128
STEPS = 4
RIM = 8
time_step = 0.2


def iota(shape, dim):
    return lax.broadcasted_iota(I32, shape, dim)


def mm(a, b):
    return jnp.dot(a, b, preferred_element_type=F32)


def split2(x):
    high = x.astype(BF16)
    return high, (x - high.astype(F32)).astype(BF16)


def contacts(field, sel):
    high, low = split2(field)
    out = mm(jnp.concatenate([high, low], axis=0), sel)
    return out[:EL].astype(BF16), out[EL:].astype(BF16)


def send_faces(snd, chi, clo):
    out = mm(snd, chi[:, 256:768]) + mm(snd, clo[:, 256:768])
    return (
        out[0:8, 384:512],
        out[8:16, 256:384],
        out[16:24, 128:256] + out[24:32, 0:128],
    )


def setup_kernel(base_ref, nbr_any, own_any, state_any, gd_ref, snd_ref, order_ref, sel_ref, chi_ref, clo_ref, zdn_ref, zup_ref, y_ref, nbr_ref, own_ref, state_ref, sem):
    copies = [
        pltpu.make_async_copy(src, dst, sem.at[k])
        for k, (src, dst) in enumerate(((nbr_any, nbr_ref), (own_any, own_ref), (state_any, state_ref)))
    ]
    for copy in copies:
        copy.start()
    for copy in copies:
        copy.wait()
    base = base_ref[0]
    sub = iota((EL, EL), 0)
    lane = iota((EL, EL), 1)
    eye = sub == lane

    def column(row):
        return jnp.sum(jnp.where(eye, jnp.broadcast_to(row, (EL, EL)), 0), axis=1, keepdims=True)

    sends = {}
    for face in range(6):
        row = nbr_ref[face : face + 1, :]
        col = column(row)
        local = col - base
        g = jnp.where(local == lane, 1.0, 0.0)
        if face >= 2:
            out_row = jnp.where((row >= 0) & ((row < base) | (row >= base + EL)), 1, 0)
            out_col = column(out_row)
            rank_out = jnp.sum(jnp.where((out_col > 0) & (col < row), 1, 0), axis=0, keepdims=True)
            s = (rank_out == iota((RIM, EL), 0)) & (out_row > 0)
            sends[face] = jnp.where(s, 1.0, 0.0)
            rank_in = jnp.sum(jnp.where((out_row > 0) & (lane < sub), 1, 0), axis=1, keepdims=True)
            d = (rank_in == iota((EL, 16), 1)) & (out_col > 0)
            d = jnp.where(d, 1.0, 0.0)
        else:
            d = jnp.zeros((EL, 16), F32)
        gd_ref[face] = jnp.concatenate([g, d], axis=1).astype(BF16)
    snd = jnp.concatenate([sends[4], sends[5], sends[2], sends[3]], axis=0).astype(BF16)
    snd_ref[...] = snd
    own_row = own_ref[...]
    own_col = column(own_row)
    rank = jnp.sum(jnp.where((own_col == own_row) & (sub < lane), 1, 0), axis=0, keepdims=True) + HALF * own_row
    rank_col = column(rank)
    order_ref[...] = jnp.sum(jnp.where(rank_col == lane, sub, 0), axis=0, keepdims=True)
    col = iota((1, 768), 1)
    face = col // 128
    rest = col % 128
    var = rest // 16
    q = rest % 16
    slow = q // 4
    fast = q % 4
    axis = face // 2
    side = 3 * (1 - face % 2)
    node = jnp.where(
        axis == 0,
        side + 4 * fast + 16 * slow,
        jnp.where(axis == 1, fast + 4 * side + 16 * slow, fast + 4 * slow + 16 * side),
    )
    target = jnp.where(rest < 80, var * NODES + node, -1)
    sel = jnp.where(iota((C, 768), 0) == target, 1.0, 0.0).astype(BF16)
    sel_ref[...] = sel
    chi, clo = contacts(state_ref[...], sel)
    chi_ref[...] = chi
    clo_ref[...] = clo
    zdn_ref[...], zup_ref[...], y_ref[...] = send_faces(snd, chi, clo)


def prep_kernel(vol_ref, lift_ref, mass_ref, w_ref, m_ref):
    w_ref[...] = jnp.zeros_like(w_ref)
    high, low = split2(vol_ref[...])
    w_ref[0:C, 0:C] = high
    w_ref[0:C, CP : CP + C] = low
    for face in range(6):
        high, low = split2(lift_ref[face])
        start = CP + 128 * face
        w_ref[start : start + 80, 0:C] = high
        w_ref[start : start + 80, CP : CP + C] = low
    high, low = split2(mass_ref[...])
    m_ref[:, 0:NODES] = high
    m_ref[:, NODES:128] = low


def step_kernel(last, order_ref, ana_ref, field_ref, chi_ref, clo_ref, gd_ref, snd_ref, sel_ref, w_ref, m_ref, zlo_ref, zhi_ref, y_ref, *outs):
    rest = list(outs)
    new_ref = rest.pop() if last else rest.pop(0)
    field = field_ref[...]
    fhi, flo = split2(field)
    pad = jnp.zeros((EL, CP - C), BF16)
    his = [fhi, pad]
    los = [flo, pad]
    y_in = y_ref[0:RIM, 0:128]
    arrived = {2: y_in, 3: y_in, 4: zlo_ref[...], 5: zhi_ref[...]}
    for face in range(6):
        lanes = slice(128 * face, 128 * face + 128)
        rows = jnp.concatenate([chi_ref[:, lanes], clo_ref[:, lanes]], axis=1)
        if face >= 2:
            ahi, alo = split2(jnp.concatenate([arrived[face], jnp.zeros((8, 128), F32)], axis=0))
            rows = jnp.concatenate([rows, jnp.concatenate([ahi, alo], axis=1)], axis=0)
            picked = mm(gd_ref[face], rows)
        else:
            picked = mm(gd_ref[face, :, 0:EL], rows)
        his.append(picked[:, 0:128].astype(BF16))
        los.append(picked[:, 128:256].astype(BF16))
    both = jnp.concatenate([jnp.concatenate(his, axis=1), jnp.concatenate(los, axis=1)], axis=0)
    prod = mm(both, w_ref[...])
    tend = (prod[:EL, 0:C] + prod[EL:, 0:C]) + (prod[:EL, CP : CP + C] + prod[EL:, CP : CP + C])
    own_block = iota((HALF, 1024), 1) // NODES == iota((HALF, 1024), 0)
    parts = []
    for tile in range(2):
        his = []
        los = []
        for var in range(5):
            one = tend[HALF * tile : HALF * tile + HALF, NODES * var : NODES * var + NODES]
            wide = jnp.concatenate([one, one], axis=1)
            wide = jnp.concatenate([wide] * 8, axis=1)
            high, low = split2(jnp.where(own_block, wide, 0.0))
            his.append(high)
            los.append(low)
        left = jnp.concatenate(his + los, axis=0)
        prod = mm(left, m_ref[1024 * tile : 1024 * tile + 1024, :])
        prod = prod[0:80] + prod[80:160]
        prod = prod[:, 0:NODES] + prod[:, NODES:128]
        parts.append(jnp.concatenate([prod[HALF * var : HALF * var + HALF] for var in range(5)], axis=1))
    new = field + time_step * jnp.concatenate(parts, axis=0)
    new_ref[...] = new
    ana = ana_ref[0]
    if last:
        fown_ref, fsend_ref = rest
        first = 0
    else:
        chi_out, clo_out, zdn_ref, zup_ref, fsend_ref, fown_ref = rest
        first = RIM
        chi, clo = contacts(new, sel_ref[...])
        chi_out[...] = chi
        clo_out[...] = clo
        zdn, zup, y = send_faces(snd_ref[...], chi, clo)
        zdn_ref[...] = zdn
        zup_ref[...] = zup
        fsend_ref[0:RIM, 0:128] = y
        fsend_ref[0:RIM, 128:CP] = jnp.zeros((RIM, CP - 128), F32)
    fsend_ref[first : first + HALF, C:CP] = jnp.zeros((HALF, CP - C), F32)
    fown_ref[:, C:CP] = jnp.zeros((HALF, CP - C), F32)
    for k in range(HALF):
        mine = order_ref[0, ana * HALF + k]
        other = order_ref[0, (1 - ana) * HALF + k]
        fown_ref[k : k + 1, 0:C] = new_ref[pl.ds(mine, 1), :]
        fsend_ref[first + k : first + k + 1, 0:C] = new_ref[pl.ds(other, 1), :]


def pick_kernel(order_ref, ana_ref, hist_ref, keep_ref, sent_ref, sem):
    ana = ana_ref[0]
    copies = []
    for k in range(HALF):
        copies.append(pltpu.make_async_copy(hist_ref.at[order_ref[0, ana * HALF + k]], keep_ref.at[k], sem.at[k]))
        copies.append(
            pltpu.make_async_copy(hist_ref.at[order_ref[0, (1 - ana) * HALF + k]], sent_ref.at[k], sem.at[HALF + k])
        )
    for copy in copies:
        copy.start()
    for copy in copies:
        copy.wait()


def gram_kernel(keep_ref, sent_ref, mine_ref, theirs_ref):
    for ref, out_ref in ((keep_ref, mine_ref), (sent_ref, theirs_ref)):
        total = None
        for k in range(0, HALF, 4):
            rows = ref[k : k + 4].reshape(4 * C, HIST)
            part = lax.dot_general(rows, rows, (((0,), (0,)), ((), ())), preferred_element_type=F32)
            total = part if total is None else total + part
        out_ref[...] = jnp.zeros_like(out_ref)
        out_ref[0:HIST, 0:HIST] = total


def factor_kernel(scale, gram_ref, up_ref, inv_ref):
    tiles = SNAPS // 8
    row = iota((SNAPS, SNAPS), 0)
    col = iota((SNAPS, SNAPS), 1)
    start = jnp.where((row < HIST) & (col < HIST), gram_ref[...] * scale, jnp.where(row == col, 1.0, 0.0))
    ident = jnp.where(row == col, 1.0, 0.0)
    a = [start[8 * t : 8 * t + 8] for t in range(tiles)]
    b = [ident[8 * t : 8 * t + 8] for t in range(tiles)]
    below = iota((8, SNAPS), 0)
    for j in range(0, HIST, 2):
        t = j // 8
        r = j % 8
        a0 = a[t][r : r + 1, :]
        a1 = a[t][r + 1 : r + 2, :]
        b0 = b[t][r : r + 1, :]
        b1 = b[t][r + 1 : r + 2, :]
        p = a0[:, j : j + 1]
        q = a0[:, j + 1 : j + 2]
        s = a1[:, j + 1 : j + 2]
        inv = 1.0 / (p * s - q * q)
        ip = jnp.broadcast_to(s * inv, (1, SNAPS))
        iq = jnp.broadcast_to(q * inv, (1, SNAPS))
        js = jnp.broadcast_to(p * inv, (1, SNAPS))
        sa0 = jnp.broadcast_to(ip * a0 - iq * a1, (8, SNAPS))
        sa1 = jnp.broadcast_to(js * a1 - iq * a0, (8, SNAPS))
        sb0 = jnp.broadcast_to(ip * b0 - iq * b1, (8, SNAPS))
        sb1 = jnp.broadcast_to(js * b1 - iq * b0, (8, SNAPS))
        for k in range(t, tiles):
            if k == t and r == 6:
                continue
            m0 = jnp.broadcast_to(a[k][:, j : j + 1], (8, SNAPS))
            m1 = jnp.broadcast_to(a[k][:, j + 1 : j + 2], (8, SNAPS))
            if k == t:
                m0 = jnp.where(below > r + 1, m0, 0.0)
                m1 = jnp.where(below > r + 1, m1, 0.0)
            a[k] = a[k] - m0 * sa0 - m1 * sa1
            b[k] = b[k] - m0 * sb0 - m1 * sb1
    up = jnp.concatenate(a, axis=0)
    low = jnp.concatenate(b, axis=0)
    odd = (iota((SNAPS, 1), 0) % 2) == 1
    diag = jnp.sum(jnp.where(row == col, up, 0.0), axis=1, keepdims=True)
    side = jnp.sum(jnp.where(row == col + 1, up, 0.0), axis=1, keepdims=True)
    before = pltpu.roll(jnp.broadcast_to(diag, (SNAPS, SNAPS)), 1, 0)[:, 0:1]
    ratio = jnp.where(odd, side / before, 0.0)
    root = 1.0 / jnp.sqrt(diag - ratio * side)
    up = (up - ratio * pltpu.roll(up, 1, 0)) * root
    low = (low - ratio * pltpu.roll(low, 1, 0)) * root
    up_ref[...] = jnp.where(col >= row, up, 0.0)
    inv_ref[...] = jnp.where(col <= row, low, 0.0)


def rows_kernel(fields_ref, keep_ref, other_ref, out_ref, turned_ref):
    f = fields_ref[...]
    high = f.astype(BF16).astype(F32)
    mid = (f - high).astype(BF16).astype(F32)
    low = f - high - mid
    zero = jnp.zeros((4, C), F32)
    total = None
    for half, ref in ((0, keep_ref), (1, other_ref)):
        for k in range(HALF):
            at = slice(64 * half + 4 * k, 64 * half + 4 * k + 4)
            left = jnp.concatenate([high[at, 0:C], mid[at, 0:C], low[at, 0:C], zero], axis=0).astype(BF16)
            part = mm(left, ref[k])
            total = part if total is None else total + part
    rows = total[0:4] + total[4:8] + total[8:12]
    rows = jnp.concatenate([rows, jnp.zeros((4, 4), F32)], axis=1)
    lane = iota((4, SNAPS), 1)
    sub = iota((4, SNAPS), 0)
    for d in range(STEPS):
        other = f if d == 0 else pltpu.roll(f, SNAPS - d, 0)
        pair = jnp.sum(f * other, axis=1, keepdims=True)
        for s in range(STEPS - d):
            both = jnp.sum(jnp.where(iota((SNAPS, 1), 0) % 4 == s, pair, 0.0), axis=0, keepdims=True)
            at = (sub == s) & (lane == HIST + s + d)
            at = at | ((sub == s + d) & (lane == HIST + s))
            rows = jnp.where(at, both, rows)
    out_ref[...] = jnp.broadcast_to(rows[None], out_ref.shape)
    turned = f.T[0:C]
    high, low = split2(turned)
    turned_ref[:, 0:SNAPS] = high
    turned_ref[:, SNAPS : 2 * SNAPS] = low


def border_kernel(scale, gathered_ref, up_ref, inv_ref, w_ref, wf_ref, fac_ref):
    rows = jnp.sum(gathered_ref[...], axis=0) * scale
    lane = iota((4, SNAPS), 1)
    g21 = jnp.where(lane < HIST, rows, 0.0)
    inv = inv_ref[...]
    l21 = lax.dot_general(g21, inv, (((1,), (1,)), ((), ())), precision=HIGHEST, preferred_element_type=F32)
    l21 = jnp.where(lane < HIST, l21, 0.0)
    comp = [[None] * 4 for _ in range(4)]
    for s in range(4):
        for u in range(s, 4):
            g = jnp.sum(jnp.where(lane[0:1] == HIST + u, rows[s : s + 1], 0.0), axis=1, keepdims=True)
            comp[s][u] = g - jnp.sum(l21[s : s + 1] * l21[u : u + 1], axis=1, keepdims=True)
    tail = lax.dot_general(l21, inv, (((1,), (0,)), ((), ())), precision=HIGHEST, preferred_element_type=F32)
    unit = jnp.where(lane == iota((4, SNAPS), 0) + HIST, 1.0, 0.0)
    work = [unit[s : s + 1] - tail[s : s + 1] for s in range(4)]
    ups = []
    outs = []
    for s in range(4):
        root = 1.0 / jnp.sqrt(comp[s][s])
        urow = [None] * 4
        for u in range(s, 4):
            urow[u] = comp[s][u] * root
        ups.append(urow)
        outs.append(work[s] * root)
        for u in range(s + 1, 4):
            work[u] = work[u] - urow[u] * outs[s]
            for v in range(u, 4):
                comp[u][v] = comp[u][v] - urow[u] * urow[v]
    new_rows = jnp.concatenate(outs, axis=0)
    full = jnp.concatenate([inv[0:HIST], new_rows], axis=0)
    wide = full.T
    high, low = split2(wide)
    w_ref[:, 0:SNAPS] = high
    w_ref[:, SNAPS : 2 * SNAPS] = low
    ends = jnp.concatenate([high[HIST:], low[HIST:]], axis=1).astype(F32)
    ends = jnp.concatenate([ends, ends], axis=0)
    wf_ref[...] = jnp.concatenate([ends] * 32, axis=0).astype(BF16)
    tri = jnp.zeros((4, SNAPS), F32)
    sub = iota((4, SNAPS), 0)
    for s in range(4):
        for u in range(s, 4):
            tri = jnp.where((sub == s) & (lane == HIST + u), ups[s][u], tri)
    lower = up_ref[...].T
    lower = jnp.concatenate([lower[0:HIST], l21], axis=0)
    upper = lower.T
    fac_ref[0] = jnp.concatenate([upper[0:HIST], tri], axis=0)


def final_kernel(ana_ref, w_ref, wf_ref, turned_ref, keep_ref, other_ref, out_ref):
    i = pl.program_id(0)
    ana = ana_ref[0]
    main = w_ref[0:HIST, :]
    ends = wf_ref[...].astype(F32)
    turned = turned_ref[...]
    element = (iota((2 * SNAPS, 2 * SNAPS), 0) % SNAPS) // 4
    for half, which, ref in ((0, ana, keep_ref), (1, 1 - ana, other_ref)):
        for k in range(2):
            at = 2 * i + k
            tail = jnp.where(element == at + HALF * half, ends, 0.0).astype(BF16)
            prod = mm(ref[at], main) + mm(turned, tail)
            out_ref[which, k] = prod[:, 0:SNAPS] + prod[:, SNAPS : 2 * SNAPS]


def shape(dims, kind=F32):
    return jax.ShapeDtypeStruct(dims, kind)


SMEM = pl.BlockSpec(memory_space=pltpu.SMEM)
VMEM = pl.BlockSpec(memory_space=pltpu.VMEM)
ANY = pl.BlockSpec(memory_space=pl.ANY)
PARAMS = pltpu.CompilerParams(vmem_limit_bytes=40 << 20)


def body(state, history, inv_mass, vol_op, lift_ops, neighbors, owner):
    groups = lax.axis_size("solver")
    ana = lax.axis_index("ana").astype(I32)
    base = (lax.axis_index(("solver", "ana")) * EL).astype(I32).reshape(1)
    ana = ana.reshape(1)
    hist = jnp.transpose(history, (1, 2, 0))
    mass = jnp.transpose(inv_mass, (2, 0, 1)).reshape(EL * NODES, NODES)
    scale = 1.0 / (EL * C * groups)
    rise = [(i, (i + 1) % groups) for i in range(groups)]
    fall = [((i + 1) % groups, i) for i in range(groups)]
    swap = [(0, 1), (1, 0)]

    gd, snd, order, sel, chi, clo, zdn, zup, yout = pl.pallas_call(
        setup_kernel,
        in_specs=[SMEM, ANY, ANY, ANY],
        scratch_shapes=[
            pltpu.VMEM((6, EL), I32),
            pltpu.VMEM((1, EL), I32),
            pltpu.VMEM((EL, C), F32),
            pltpu.SemaphoreType.DMA((3,)),
        ],
        out_shape=(
            shape((6, EL, 48), BF16),
            shape((EL, EL), BF16),
            shape((1, EL), I32),
            shape((C, 768), BF16),
            shape((EL, 768), BF16),
            shape((EL, 768), BF16),
            shape((RIM, 128)),
            shape((RIM, 128)),
            shape((RIM, 128)),
        ),
        compiler_params=PARAMS,
        name="setup",
    )(base, neighbors, owner.reshape(1, EL), state)

    keep, sent = pl.pallas_call(
        pick_kernel,
        in_specs=[SMEM, SMEM, ANY],
        out_shape=(shape((HALF, C, HIST), BF16), shape((HALF, C, HIST), BF16)),
        scratch_shapes=[pltpu.SemaphoreType.DMA((2 * HALF,))],
        compiler_params=PARAMS,
        name="pick",
    )(order, ana, hist)
    other = lax.ppermute(sent, "ana", swap)

    w, m = pl.pallas_call(
        prep_kernel,
        in_specs=[VMEM, VMEM, VMEM],
        out_shape=(shape((CP + 768, 2 * CP), BF16), shape((EL * NODES, 128), BF16)),
        compiler_params=PARAMS,
        name="prep",
    )(vol_op, lift_ops, mass)

    gram, theirs = pl.pallas_call(
        gram_kernel,
        in_specs=[VMEM, VMEM],
        out_shape=(shape((SNAPS, SNAPS)), shape((SNAPS, SNAPS))),
        compiler_params=PARAMS,
        name="gram",
    )(keep, sent)

    field = state
    owns = []
    recvs = []
    bits = [1 << k for k in range(groups.bit_length() - 1)]
    rounds = [[0] + bits[0:1], bits[1:3], bits[3:5], bits[5:]]
    for step in range(STEPS):
        zlo = lax.ppermute(zup, "solver", rise)
        zhi = lax.ppermute(zdn, "solver", fall)
        yin = lax.ppermute(yout, "ana", swap)
        for bit in rounds[step]:
            if bit:
                gram = gram + lax.ppermute(gram, "solver", [(i, i ^ bit) for i in range(groups)])
            else:
                gram = gram + lax.ppermute(theirs, "ana", swap)
        zlo, gram = lax.optimization_barrier((zlo, gram))
        if step:
            recvs.append(yin[RIM:])
        last = step == STEPS - 1
        outs = [shape((HALF, CP))]
        if last:
            outs = outs + [shape((HALF, CP)), shape((EL, C))]
        else:
            outs = [
                shape((EL, C)),
                shape((EL, 768), BF16),
                shape((EL, 768), BF16),
                shape((RIM, 128)),
                shape((RIM, 128)),
                shape((RIM + HALF, CP)),
            ] + outs
        res = pl.pallas_call(
            functools.partial(step_kernel, last),
            in_specs=[SMEM, SMEM] + [VMEM] * 11,
            out_shape=tuple(outs),
            compiler_params=PARAMS,
            name="step",
        )(order, ana, field, chi, clo, gd, snd, sel, w, m, zlo, zhi, yin)
        if last:
            own, rows_out = res[0], res[1]
        else:
            field, chi, clo, zdn, zup, yout, own = res
        owns.append(own)
    recvs.append(lax.ppermute(rows_out, "ana", swap))
    fields = jnp.stack([jnp.stack(owns, axis=1), jnp.stack(recvs, axis=1)]).reshape(SNAPS, CP)

    up, inv = pl.pallas_call(
        functools.partial(factor_kernel, scale),
        in_specs=[VMEM],
        out_shape=(shape((SNAPS, SNAPS)), shape((SNAPS, SNAPS))),
        compiler_params=PARAMS,
        name="factor",
    )(gram)

    rows, turned = pl.pallas_call(
        rows_kernel,
        in_specs=[VMEM, VMEM, VMEM],
        out_shape=(shape((groups, STEPS, SNAPS)), shape((C, 2 * SNAPS), BF16)),
        compiler_params=PARAMS,
        name="rows",
    )(fields, keep, other)
    gathered = lax.all_to_all(rows, "solver", 0, 0, tiled=True)

    wide, wf, fac = pl.pallas_call(
        functools.partial(border_kernel, scale),
        in_specs=[VMEM, VMEM, VMEM],
        out_shape=(shape((SNAPS, 2 * SNAPS), BF16), shape((2 * SNAPS, 2 * SNAPS), BF16), shape((1, SNAPS, SNAPS))),
        compiler_params=PARAMS,
        name="border",
    )(gathered, up, inv)

    coef = pl.pallas_call(
        final_kernel,
        grid=(HALF // 2,),
        in_specs=[SMEM] + [VMEM] * 5,
        out_specs=pl.BlockSpec((2, 2, C, SNAPS), lambda i: (0, i, 0, 0)),
        out_shape=shape((2, HALF, C, SNAPS)),
        compiler_params=PARAMS,
        name="final",
    )(ana, wide, wf, turned, keep, other)
    return coef.reshape(EL, C, SNAPS), fac


def solution(mesh):
    return jax.shard_map(
        body,
        mesh=mesh,
        in_specs=(
            P(("solver", "ana"), None),
            P(None, ("solver", "ana"), None),
            P(None, None, ("solver", "ana")),
            P(),
            P(),
            P(None, ("solver", "ana")),
            P(("solver", "ana")),
        ),
        out_specs=(P(("solver", "ana"), None, None), P("ana", None, None)),
        check_vma=False,
    )
```

```python
import functools

import jax
import jax.numpy as jnp
from jax import lax
from jax.experimental import pallas as pl
from jax.experimental.pallas import tpu as pltpu
from jax.sharding import PartitionSpec as P

F32 = jnp.float32
BF16 = jnp.bfloat16
I32 = jnp.int32
HIGHEST = lax.Precision.HIGHEST

EL = 32
HALF = 16
C = 320
CP = 384
NODES = 64
HIST = 124
SNAPS = 128
STEPS = 4
FOLD = 72
FINAL = 2
RIM = 8
time_step = 0.2


def iota(shape, dim):
    return lax.broadcasted_iota(I32, shape, dim)


def mm(a, b):
    return jnp.dot(a, b, preferred_element_type=F32)


def split2(x):
    high = x.astype(BF16)
    return high, (x - high.astype(F32)).astype(BF16)


def contacts(field, sel):
    high, low = split2(field)
    out = mm(jnp.concatenate([high, low], axis=0), sel)
    return out[:EL].astype(BF16), out[EL:].astype(BF16)


def send_faces(snd, chi, clo, parity):
    out = mm(snd, chi[:, 256:768]) + mm(snd, clo[:, 256:768])
    below = out[0:8, 384:512]
    above = out[8:16, 256:384]
    even = parity == 0
    return (
        jnp.where(even, above, below),
        jnp.where(even, below, above),
        out[16:24, 128:256] + out[24:32, 0:128],
    )


def setup_kernel(base_ref, place_ref, nbr_any, own_any, state_any, gd_ref, snd_ref, order_ref, sel_ref, chi_ref, clo_ref, zev_ref, zod_ref, y_ref, nbr_ref, own_ref, state_ref, sem):
    copies = [
        pltpu.make_async_copy(src, dst, sem.at[k])
        for k, (src, dst) in enumerate(((nbr_any, nbr_ref), (own_any, own_ref), (state_any, state_ref)))
    ]
    for copy in copies:
        copy.start()
    for copy in copies:
        copy.wait()
    base = base_ref[0]
    sub = iota((EL, EL), 0)
    lane = iota((EL, EL), 1)
    eye = sub == lane

    def column(row):
        return jnp.sum(jnp.where(eye, jnp.broadcast_to(row, (EL, EL)), 0), axis=1, keepdims=True)

    sends = {}
    for face in range(6):
        row = nbr_ref[face : face + 1, :]
        col = column(row)
        local = col - base
        g = jnp.where(local == lane, 1.0, 0.0)
        if face >= 2:
            out_row = jnp.where((row >= 0) & ((row < base) | (row >= base + EL)), 1, 0)
            out_col = column(out_row)
            rank_out = jnp.sum(jnp.where((out_col > 0) & (col < row), 1, 0), axis=0, keepdims=True)
            s = (rank_out == iota((RIM, EL), 0)) & (out_row > 0)
            sends[face] = jnp.where(s, 1.0, 0.0)
            rank_in = jnp.sum(jnp.where((out_row > 0) & (lane < sub), 1, 0), axis=1, keepdims=True)
            d = (rank_in == iota((EL, 16), 1)) & (out_col > 0)
            d = jnp.where(d, 1.0, 0.0)
        else:
            d = jnp.zeros((EL, 16), F32)
        gd_ref[face] = jnp.concatenate([g, d], axis=1).astype(BF16)
    snd = jnp.concatenate([sends[4], sends[5], sends[2], sends[3]], axis=0).astype(BF16)
    snd_ref[...] = snd
    own_row = own_ref[...]
    own_col = column(own_row)
    rank = jnp.sum(jnp.where((own_col == own_row) & (sub < lane), 1, 0), axis=0, keepdims=True) + HALF * own_row
    rank_col = column(rank)
    order_ref[...] = jnp.sum(jnp.where(rank_col == lane, sub, 0), axis=0, keepdims=True)
    col = iota((1, 768), 1)
    face = col // 128
    rest = col % 128
    var = rest // 16
    q = rest % 16
    slow = q // 4
    fast = q % 4
    axis = face // 2
    side = 3 * (1 - face % 2)
    node = jnp.where(
        axis == 0,
        side + 4 * fast + 16 * slow,
        jnp.where(axis == 1, fast + 4 * side + 16 * slow, fast + 4 * slow + 16 * side),
    )
    target = jnp.where(rest < 80, var * NODES + node, -1)
    sel = jnp.where(iota((C, 768), 0) == target, 1.0, 0.0).astype(BF16)
    sel_ref[...] = sel
    chi, clo = contacts(state_ref[...], sel)
    chi_ref[...] = chi
    clo_ref[...] = clo
    zev_ref[...], zod_ref[...], y_ref[...] = send_faces(snd, chi, clo, place_ref[1])


def prep_kernel(vol_ref, lift_ref, mass_ref, w_ref, m_ref):
    w_ref[...] = jnp.zeros_like(w_ref)
    high, low = split2(vol_ref[...])
    w_ref[0:C, 0:C] = high
    w_ref[0:C, CP : CP + C] = low
    for face in range(6):
        high, low = split2(lift_ref[face])
        start = CP + 128 * face
        w_ref[start : start + 80, 0:C] = high
        w_ref[start : start + 80, CP : CP + C] = low
    high, low = split2(mass_ref[...])
    m_ref[:, 0:NODES] = high
    m_ref[:, NODES:128] = low


def step_kernel(last, order_ref, place_ref, field_ref, chi_ref, clo_ref, gd_ref, snd_ref, sel_ref, w_ref, m_ref, even_ref, odd_ref, y_ref, *outs):
    rest = list(outs)
    new_ref = rest.pop() if last else rest.pop(0)
    field = field_ref[...]
    fhi, flo = split2(field)
    pad = jnp.zeros((EL, CP - C), BF16)
    his = [fhi, pad]
    los = [flo, pad]
    y_in = y_ref[0:RIM, 0:128]
    even = place_ref[1] == 0
    by_even = even_ref[0:RIM]
    by_odd = odd_ref[...]
    arrived = {2: y_in, 3: y_in, 4: jnp.where(even, by_odd, by_even), 5: jnp.where(even, by_even, by_odd)}
    for face in range(6):
        lanes = slice(128 * face, 128 * face + 128)
        rows = jnp.concatenate([chi_ref[:, lanes], clo_ref[:, lanes]], axis=1)
        if face >= 2:
            ahi, alo = split2(jnp.concatenate([arrived[face], jnp.zeros((8, 128), F32)], axis=0))
            rows = jnp.concatenate([rows, jnp.concatenate([ahi, alo], axis=1)], axis=0)
            picked = mm(gd_ref[face], rows)
        else:
            picked = mm(gd_ref[face, :, 0:EL], rows)
        his.append(picked[:, 0:128].astype(BF16))
        los.append(picked[:, 128:256].astype(BF16))
    both = jnp.concatenate([jnp.concatenate(his, axis=1), jnp.concatenate(los, axis=1)], axis=0)
    prod = mm(both, w_ref[...])
    tend = (prod[:EL, 0:C] + prod[EL:, 0:C]) + (prod[:EL, CP : CP + C] + prod[EL:, CP : CP + C])
    own_block = iota((HALF, 1024), 1) // NODES == iota((HALF, 1024), 0)
    parts = []
    for tile in range(2):
        his = []
        los = []
        for var in range(5):
            one = tend[HALF * tile : HALF * tile + HALF, NODES * var : NODES * var + NODES]
            wide = jnp.concatenate([one, one], axis=1)
            wide = jnp.concatenate([wide] * 8, axis=1)
            high, low = split2(jnp.where(own_block, wide, 0.0))
            his.append(high)
            los.append(low)
        left = jnp.concatenate(his + los, axis=0)
        prod = mm(left, m_ref[1024 * tile : 1024 * tile + 1024, :])
        prod = prod[0:80] + prod[80:160]
        prod = prod[:, 0:NODES] + prod[:, NODES:128]
        parts.append(jnp.concatenate([prod[HALF * var : HALF * var + HALF] for var in range(5)], axis=1))
    new = field + time_step * jnp.concatenate(parts, axis=0)
    new_ref[...] = new
    ana = place_ref[0]
    if last:
        fown_ref, fsend_ref = rest
        first = 0
    else:
        chi_out, clo_out, zev_ref, zod_ref, fsend_ref, fown_ref = rest
        first = RIM
        chi, clo = contacts(new, sel_ref[...])
        chi_out[...] = chi
        clo_out[...] = clo
        zev, zod, y = send_faces(snd_ref[...], chi, clo, place_ref[1])
        zev_ref[...] = zev
        zod_ref[...] = zod
        fsend_ref[0:RIM, 0:128] = y
        fsend_ref[0:RIM, 128:CP] = jnp.zeros((RIM, CP - 128), F32)
    fsend_ref[first : first + HALF, C:CP] = jnp.zeros((HALF, CP - C), F32)
    fown_ref[:, C:CP] = jnp.zeros((HALF, CP - C), F32)
    for k in range(HALF):
        mine = order_ref[0, ana * HALF + k]
        other = order_ref[0, (1 - ana) * HALF + k]
        fown_ref[k : k + 1, 0:C] = new_ref[pl.ds(mine, 1), :]
        fsend_ref[first + k : first + k + 1, 0:C] = new_ref[pl.ds(other, 1), :]


def pick_kernel(order_ref, place_ref, hist_ref, keep_ref, sent_ref, sem):
    ana = place_ref[0]
    copies = []
    for k in range(HALF):
        copies.append(pltpu.make_async_copy(hist_ref.at[order_ref[0, ana * HALF + k]], keep_ref.at[k], sem.at[k]))
        copies.append(
            pltpu.make_async_copy(hist_ref.at[order_ref[0, (1 - ana) * HALF + k]], sent_ref.at[k], sem.at[HALF + k])
        )
    for copy in copies:
        copy.start()
    for copy in copies:
        copy.wait()


def gram_kernel(keep_ref, sent_ref, mine_ref, theirs_ref, full_ref):
    row = iota((64, SNAPS), 0)
    col = iota((64, SNAPS), 1)
    for ref, out_ref in ((keep_ref, mine_ref), (sent_ref, theirs_ref)):
        total = None
        for k in range(0, HALF, 4):
            rows = ref[k : k + 4].reshape(4 * C, HIST)
            part = lax.dot_general(rows, rows, (((0,), (0,)), ((), ())), preferred_element_type=F32)
            total = part if total is None else total + part
        full_ref[...] = jnp.zeros_like(full_ref)
        full_ref[0:HIST, 0:HIST] = total
        last = pltpu.roll(full_ref[64:SNAPS], 64, 1)
        out_ref[0:64] = jnp.where(col < row, last, full_ref[0:64])
        diag = jnp.sum(jnp.where(col == row, last, 0.0), axis=0, keepdims=True)
        out_ref[64:FOLD] = jnp.broadcast_to(diag, (FOLD - 64, SNAPS))


def unfold(folded):
    row = iota((64, SNAPS), 0)
    col = iota((64, SNAPS), 1)
    top = folded[0:64]
    upper = jnp.where(col > row, top, 0.0)
    lower = pltpu.roll(jnp.where(col < row, top, 0.0), 64, 1)
    half = jnp.concatenate([upper, lower], axis=0)
    last = pltpu.roll(jnp.broadcast_to(folded[64:65], (64, SNAPS)), 64, 1)
    diag = jnp.concatenate([jnp.where(col == row, top, 0.0), jnp.where(col == row + 64, last, 0.0)], axis=0)
    return half + half.T + diag


def factor_kernel(scale, gram_ref, up_ref, inv_ref):
    tiles = SNAPS // 8
    row = iota((SNAPS, SNAPS), 0)
    col = iota((SNAPS, SNAPS), 1)
    start = jnp.where((row < HIST) & (col < HIST), unfold(gram_ref[...]) * scale, jnp.where(row == col, 1.0, 0.0))
    ident = jnp.where(row == col, 1.0, 0.0)
    a = [start[8 * t : 8 * t + 8] for t in range(tiles)]
    b = [ident[8 * t : 8 * t + 8] for t in range(tiles)]
    below = iota((8, SNAPS), 0)
    full = (8, SNAPS)
    for j in range(0, HIST, 2):
        t = j // 8
        r = j % 8
        m0 = {k: jnp.broadcast_to(a[k][:, j : j + 1], full) for k in range(t, tiles)}
        m1 = {k: jnp.broadcast_to(a[k][:, j + 1 : j + 2], full) for k in range(t, tiles)}
        p = jnp.broadcast_to(m0[t][r : r + 1], full)
        q = jnp.broadcast_to(m0[t][r + 1 : r + 2], full)
        s = jnp.broadcast_to(m1[t][r + 1 : r + 2], full)
        a0 = jnp.broadcast_to(a[t][r : r + 1], full)
        a1 = jnp.broadcast_to(a[t][r + 1 : r + 2], full)
        b0 = jnp.broadcast_to(b[t][r : r + 1], full)
        b1 = jnp.broadcast_to(b[t][r + 1 : r + 2], full)
        inv = 1.0 / (p * s - q * q)
        ip = s * inv
        iq = q * inv
        js = p * inv
        sa0 = ip * a0 - iq * a1
        sa1 = js * a1 - iq * a0
        sb0 = ip * b0 - iq * b1
        sb1 = js * b1 - iq * b0
        for k in range(t, tiles):
            if k == t:
                if r == 6:
                    continue
                m0[k] = jnp.where(below > r + 1, m0[k], 0.0)
                m1[k] = jnp.where(below > r + 1, m1[k], 0.0)
            a[k] = a[k] - m0[k] * sa0 - m1[k] * sa1
            b[k] = b[k] - m0[k] * sb0 - m1[k] * sb1
    up = jnp.concatenate(a, axis=0)
    low = jnp.concatenate(b, axis=0)
    odd = (iota((SNAPS, 1), 0) % 2) == 1
    diag = jnp.sum(jnp.where(row == col, up, 0.0), axis=1, keepdims=True)
    side = jnp.sum(jnp.where(row == col + 1, up, 0.0), axis=1, keepdims=True)
    before = pltpu.roll(jnp.broadcast_to(diag, (SNAPS, SNAPS)), 1, 0)[:, 0:1]
    ratio = jnp.where(odd, side / before, 0.0)
    root = 1.0 / jnp.sqrt(diag - ratio * side)
    up = (up - ratio * pltpu.roll(up, 1, 0)) * root
    low = (low - ratio * pltpu.roll(low, 1, 0)) * root
    up_ref[...] = jnp.where(col >= row, up, 0.0)
    inv_ref[...] = jnp.where(col <= row, low, 0.0)


def rows_kernel(fields_ref, keep_ref, other_ref, out_ref, turned_ref):
    f = fields_ref[...]
    high = f.astype(BF16).astype(F32)
    mid = (f - high).astype(BF16).astype(F32)
    low = f - high - mid
    zero = jnp.zeros((4, C), F32)
    total = None
    for half, ref in ((0, keep_ref), (1, other_ref)):
        for k in range(HALF):
            at = slice(64 * half + 4 * k, 64 * half + 4 * k + 4)
            left = jnp.concatenate([high[at, 0:C], mid[at, 0:C], low[at, 0:C], zero], axis=0).astype(BF16)
            part = mm(left, ref[k])
            total = part if total is None else total + part
    rows = total[0:4] + total[4:8] + total[8:12]
    rows = jnp.concatenate([rows, jnp.zeros((4, 4), F32)], axis=1)
    lane = iota((4, SNAPS), 1)
    sub = iota((4, SNAPS), 0)
    for d in range(STEPS):
        other = f if d == 0 else pltpu.roll(f, SNAPS - d, 0)
        pair = jnp.sum(f * other, axis=1, keepdims=True)
        for s in range(STEPS - d):
            both = jnp.sum(jnp.where(iota((SNAPS, 1), 0) % 4 == s, pair, 0.0), axis=0, keepdims=True)
            at = (sub == s) & (lane == HIST + s + d)
            at = at | ((sub == s + d) & (lane == HIST + s))
            rows = jnp.where(at, both, rows)
    out_ref[...] = jnp.broadcast_to(rows[None], out_ref.shape)
    turned = f.T[0:C]
    high, low = split2(turned)
    turned_ref[:, 0:SNAPS] = high
    turned_ref[:, SNAPS : 2 * SNAPS] = low


def border_kernel(scale, gathered_ref, up_ref, inv_ref, w_ref, wf_ref, fac_ref):
    rows = jnp.sum(gathered_ref[...], axis=0) * scale
    lane = iota((4, SNAPS), 1)
    g21 = jnp.where(lane < HIST, rows, 0.0)
    inv = inv_ref[...]
    l21 = lax.dot_general(g21, inv, (((1,), (1,)), ((), ())), precision=HIGHEST, preferred_element_type=F32)
    l21 = jnp.where(lane < HIST, l21, 0.0)
    comp = [[None] * 4 for _ in range(4)]
    for s in range(4):
        for u in range(s, 4):
            g = jnp.sum(jnp.where(lane[0:1] == HIST + u, rows[s : s + 1], 0.0), axis=1, keepdims=True)
            comp[s][u] = g - jnp.sum(l21[s : s + 1] * l21[u : u + 1], axis=1, keepdims=True)
    tail = lax.dot_general(l21, inv, (((1,), (0,)), ((), ())), precision=HIGHEST, preferred_element_type=F32)
    unit = jnp.where(lane == iota((4, SNAPS), 0) + HIST, 1.0, 0.0)
    work = [unit[s : s + 1] - tail[s : s + 1] for s in range(4)]
    ups = []
    outs = []
    for s in range(4):
        root = 1.0 / jnp.sqrt(comp[s][s])
        urow = [None] * 4
        for u in range(s, 4):
            urow[u] = comp[s][u] * root
        ups.append(urow)
        outs.append(work[s] * root)
        for u in range(s + 1, 4):
            work[u] = work[u] - urow[u] * outs[s]
            for v in range(u, 4):
                comp[u][v] = comp[u][v] - urow[u] * urow[v]
    new_rows = jnp.concatenate(outs, axis=0)
    full = jnp.concatenate([inv[0:HIST], new_rows], axis=0)
    wide = full.T
    high, low = split2(wide)
    w_ref[:, 0:SNAPS] = high
    w_ref[:, SNAPS : 2 * SNAPS] = low
    ends = jnp.concatenate([high[HIST:], low[HIST:]], axis=1).astype(F32)
    ends = jnp.concatenate([ends, ends], axis=0)
    wf_ref[...] = jnp.concatenate([ends] * 32, axis=0).astype(BF16)
    tri = jnp.zeros((4, SNAPS), F32)
    sub = iota((4, SNAPS), 0)
    for s in range(4):
        for u in range(s, 4):
            tri = jnp.where((sub == s) & (lane == HIST + u), ups[s][u], tri)
    lower = up_ref[...].T
    lower = jnp.concatenate([lower[0:HIST], l21], axis=0)
    upper = lower.T
    fac_ref[0] = jnp.concatenate([upper[0:HIST], tri], axis=0)


def final_kernel(place_ref, w_ref, wf_ref, turned_ref, keep_ref, other_ref, out_ref, buf_ref, sem):
    ana = place_ref[0]
    main = w_ref[0:HIST, :]
    ends = wf_ref[...]
    turned = turned_ref[...]
    element = (iota((1, 2 * SNAPS), 1) % SNAPS) // 4
    copies = []
    for at in range(0, HALF, FINAL):
        for half, which, ref in ((0, ana, keep_ref), (1, 1 - ana, other_ref)):
            own = [
                turned * jnp.where(element == at + k + HALF * half, 1.0, 0.0).astype(BF16) for k in range(FINAL)
            ]
            rows = ref[at : at + FINAL].reshape(FINAL * C, HIST)
            prod = mm(rows, main) + mm(jnp.concatenate(own, axis=0), ends)
            prod = (prod[:, 0:SNAPS] + prod[:, SNAPS : 2 * SNAPS]).reshape(FINAL, C, SNAPS)
            buf_ref[half, at : at + FINAL] = prod
            copy = pltpu.make_async_copy(
                buf_ref.at[half, pl.ds(at, FINAL)],
                out_ref.at[which, pl.ds(at, FINAL)],
                sem.at[len(copies)],
            )
            copy.start()
            copies.append(copy)
    for copy in copies:
        copy.wait()


def shape(dims, kind=F32):
    return jax.ShapeDtypeStruct(dims, kind)


SMEM = pl.BlockSpec(memory_space=pltpu.SMEM)
VMEM = pl.BlockSpec(memory_space=pltpu.VMEM)
ANY = pl.BlockSpec(memory_space=pltpu.HBM)
PARAMS = pltpu.CompilerParams(vmem_limit_bytes=40 << 20)


def in_hbm(x):
    return pltpu.with_memory_space_constraint(x, pltpu.HBM)


def body(state, history, inv_mass, vol_op, lift_ops, neighbors, owner):
    groups = lax.axis_size("solver")
    place = jnp.stack([lax.axis_index("ana"), lax.axis_index("solver") % 2]).astype(I32)
    base = (lax.axis_index(("solver", "ana")) * EL).astype(I32).reshape(1)
    hist = in_hbm(jnp.transpose(history, (1, 2, 0)))
    mass = jnp.transpose(inv_mass, (2, 0, 1)).reshape(EL * NODES, NODES)
    scale = 1.0 / (EL * C * groups)
    evens = [(i, i ^ 1) for i in range(groups)]
    odds = [(i, (i + 1 if i % 2 else i - 1) % groups) for i in range(groups)]
    swap = [(0, 1), (1, 0)]

    gd, snd, order, sel, chi, clo, zev, zod, yout = pl.pallas_call(
        setup_kernel,
        in_specs=[SMEM, SMEM, ANY, ANY, ANY],
        scratch_shapes=[
            pltpu.VMEM((6, EL), I32),
            pltpu.VMEM((1, EL), I32),
            pltpu.VMEM((EL, C), F32),
            pltpu.SemaphoreType.DMA((3,)),
        ],
        out_shape=(
            shape((6, EL, 48), BF16),
            shape((EL, EL), BF16),
            shape((1, EL), I32),
            shape((C, 768), BF16),
            shape((EL, 768), BF16),
            shape((EL, 768), BF16),
            shape((RIM, 128)),
            shape((RIM, 128)),
            shape((RIM, 128)),
        ),
        compiler_params=PARAMS,
        name="setup",
    )(base, place, in_hbm(neighbors), in_hbm(owner.reshape(1, EL)), in_hbm(state))

    keep, sent = pl.pallas_call(
        pick_kernel,
        in_specs=[SMEM, SMEM, ANY],
        out_shape=(shape((HALF, C, HIST), BF16), shape((HALF, C, HIST), BF16)),
        scratch_shapes=[pltpu.SemaphoreType.DMA((2 * HALF,))],
        compiler_params=PARAMS,
        name="pick",
    )(order, place, hist)
    w, m = pl.pallas_call(
        prep_kernel,
        in_specs=[VMEM, VMEM, VMEM],
        out_shape=(shape((CP + 768, 2 * CP), BF16), shape((EL * NODES, 128), BF16)),
        compiler_params=PARAMS,
        name="prep",
    )(vol_op, lift_ops, mass)

    gram, theirs = pl.pallas_call(
        gram_kernel,
        in_specs=[VMEM, VMEM],
        out_shape=(shape((FOLD, SNAPS)), shape((FOLD, SNAPS))),
        scratch_shapes=[pltpu.VMEM((SNAPS, SNAPS), F32)],
        compiler_params=PARAMS,
        name="gram",
    )(keep, sent)
    field = state
    owns = []
    recvs = []
    bits = [1 << k for k in range(groups.bit_length() - 1)]
    stages = [[], bits[1:3], bits[3:5], bits[5:7], bits[0:1]]

    def summed(gram, two):
        total = gram
        if not two:
            return gram
        for bit in two + ([two[0] | two[1]] if len(two) == 2 else []):
            total = total + lax.ppermute(gram, "solver", [(i, i ^ bit) for i in range(groups)])
        return total

    for step in range(STEPS):
        even = lax.ppermute(zev, "solver", evens)
        gram = summed(gram, stages[step])
        odd = lax.ppermute(zod, "solver", odds)
        yin = lax.ppermute(yout, "ana", swap)
        if step == 0:
            theirs, sent, even, odd, yin = lax.optimization_barrier((theirs, sent, even, odd, yin))
            gram = gram + lax.ppermute(theirs, "ana", swap)
            other = lax.ppermute(sent, "ana", swap)
        else:
            even, odd, yin, gram, other = lax.optimization_barrier((even, odd, yin, gram, other))
        if step:
            recvs.append(yin[RIM:])
        last = step == STEPS - 1
        outs = [shape((HALF, CP))]
        if last:
            outs = outs + [shape((HALF, CP)), shape((EL, C))]
        else:
            outs = [
                shape((EL, C)),
                shape((EL, 768), BF16),
                shape((EL, 768), BF16),
                shape((RIM, 128)),
                shape((RIM, 128)),
                shape((RIM + HALF, CP)),
            ] + outs
        res = pl.pallas_call(
            functools.partial(step_kernel, last),
            in_specs=[SMEM, SMEM] + [VMEM] * 11,
            out_shape=tuple(outs),
            compiler_params=PARAMS,
            name="step",
        )(order, place, field, chi, clo, gd, snd, sel, w, m, even, odd, yin)
        if last:
            own, rows_out = res[0], res[1]
        else:
            field, chi, clo, zev, zod, yout, own = res
            gram, zev, zod, yout = lax.optimization_barrier((gram, zev, zod, yout))
        owns.append(own)
    recvs.append(lax.ppermute(rows_out, "ana", swap))
    fields = jnp.stack([jnp.stack(owns, axis=1), jnp.stack(recvs, axis=1)]).reshape(SNAPS, CP)

    gram = summed(gram, stages[STEPS])
    up, inv = pl.pallas_call(
        functools.partial(factor_kernel, scale),
        in_specs=[VMEM],
        out_shape=(shape((SNAPS, SNAPS)), shape((SNAPS, SNAPS))),
        compiler_params=PARAMS,
        name="factor",
    )(gram)

    rows, turned = pl.pallas_call(
        rows_kernel,
        in_specs=[VMEM, VMEM, VMEM],
        out_shape=(shape((groups, STEPS, SNAPS)), shape((C, 2 * SNAPS), BF16)),
        compiler_params=PARAMS,
        name="rows",
    )(fields, keep, other)
    gathered = lax.all_to_all(rows, "solver", 0, 0, tiled=True)

    wide, wf, fac = pl.pallas_call(
        functools.partial(border_kernel, scale),
        in_specs=[VMEM, VMEM, VMEM],
        out_shape=(shape((SNAPS, 2 * SNAPS), BF16), shape((2 * SNAPS, 2 * SNAPS), BF16), shape((1, SNAPS, SNAPS))),
        compiler_params=PARAMS,
        name="border",
    )(gathered, up, inv)

    coef = pl.pallas_call(
        final_kernel,
        in_specs=[SMEM] + [VMEM] * 5,
        out_specs=ANY,
        out_shape=shape((2, HALF, C, SNAPS)),
        scratch_shapes=[
            pltpu.VMEM((2, HALF, C, SNAPS), F32),
            pltpu.SemaphoreType.DMA((2 * HALF // FINAL,)),
        ],
        compiler_params=PARAMS,
        name="final",
    )(place, wide, wf, turned, keep, other)
    return coef.reshape(EL, C, SNAPS), fac


def solution(mesh):
    return jax.shard_map(
        body,
        mesh=mesh,
        in_specs=(
            P(("solver", "ana"), None),
            P(None, ("solver", "ana"), None),
            P(None, None, ("solver", "ana")),
            P(),
            P(),
            P(None, ("solver", "ana")),
            P(("solver", "ana")),
        ),
        out_specs=(P(("solver", "ana"), None, None), P("ana", None, None)),
        check_vma=False,
    )
```

```python
import functools

import jax
import jax.numpy as jnp
from jax import lax
from jax.experimental import pallas as pl
from jax.experimental.pallas import tpu as pltpu
from jax.sharding import PartitionSpec as P

F32 = jnp.float32
BF16 = jnp.bfloat16
I32 = jnp.int32
HIGHEST = lax.Precision.HIGHEST

EL = 32
HALF = 16
C = 320
CP = 384
NODES = 64
HIST = 124
SNAPS = 128
STEPS = 4
FOLD = 72
FINAL = 2
RIM = 8
time_step = 0.2


def iota(shape, dim):
    return lax.broadcasted_iota(I32, shape, dim)


def mm(a, b):
    return jnp.dot(a, b, preferred_element_type=F32)


def split2(x):
    high = x.astype(BF16)
    return high, (x - high.astype(F32)).astype(BF16)


def contacts(field, sel):
    high, low = split2(field)
    out = mm(jnp.concatenate([high, low], axis=0), sel)
    return out[:EL].astype(BF16), out[EL:].astype(BF16)


def send_faces(snd, chi, clo, parity):
    out = mm(snd, chi[:, 256:768]) + mm(snd, clo[:, 256:768])
    below = out[0:8, 384:512]
    above = out[8:16, 256:384]
    even = parity == 0
    return (
        jnp.where(even, above, below),
        jnp.where(even, below, above),
        out[16:24, 128:256] + out[24:32, 0:128],
    )


def setup_kernel(base_ref, place_ref, nbr_any, own_any, state_any, gd_ref, snd_ref, order_ref, sel_ref, chi_ref, clo_ref, zev_ref, zod_ref, y_ref, nbr_ref, own_ref, state_ref, sem):
    copies = [
        pltpu.make_async_copy(src, dst, sem.at[k])
        for k, (src, dst) in enumerate(((nbr_any, nbr_ref), (own_any, own_ref), (state_any, state_ref)))
    ]
    for copy in copies:
        copy.start()
    for copy in copies:
        copy.wait()
    base = base_ref[0]
    sub = iota((EL, EL), 0)
    lane = iota((EL, EL), 1)
    eye = sub == lane

    def column(row):
        return jnp.sum(jnp.where(eye, jnp.broadcast_to(row, (EL, EL)), 0), axis=1, keepdims=True)

    sends = {}
    for face in range(6):
        row = nbr_ref[face : face + 1, :]
        col = column(row)
        local = col - base
        g = jnp.where(local == lane, 1.0, 0.0)
        if face >= 2:
            out_row = jnp.where((row >= 0) & ((row < base) | (row >= base + EL)), 1, 0)
            out_col = column(out_row)
            rank_out = jnp.sum(jnp.where((out_col > 0) & (col < row), 1, 0), axis=0, keepdims=True)
            s = (rank_out == iota((RIM, EL), 0)) & (out_row > 0)
            sends[face] = jnp.where(s, 1.0, 0.0)
            rank_in = jnp.sum(jnp.where((out_row > 0) & (lane < sub), 1, 0), axis=1, keepdims=True)
            d = (rank_in == iota((EL, 16), 1)) & (out_col > 0)
            d = jnp.where(d, 1.0, 0.0)
        else:
            d = jnp.zeros((EL, 16), F32)
        gd_ref[face] = jnp.concatenate([g, d], axis=1).astype(BF16)
    snd = jnp.concatenate([sends[4], sends[5], sends[2], sends[3]], axis=0).astype(BF16)
    snd_ref[...] = snd
    own_row = own_ref[...]
    own_col = column(own_row)
    rank = jnp.sum(jnp.where((own_col == own_row) & (sub < lane), 1, 0), axis=0, keepdims=True) + HALF * own_row
    rank_col = column(rank)
    order_ref[...] = jnp.sum(jnp.where(rank_col == lane, sub, 0), axis=0, keepdims=True)
    col = iota((1, 768), 1)
    face = col // 128
    rest = col % 128
    var = rest // 16
    q = rest % 16
    slow = q // 4
    fast = q % 4
    axis = face // 2
    side = 3 * (1 - face % 2)
    node = jnp.where(
        axis == 0,
        side + 4 * fast + 16 * slow,
        jnp.where(axis == 1, fast + 4 * side + 16 * slow, fast + 4 * slow + 16 * side),
    )
    target = jnp.where(rest < 80, var * NODES + node, -1)
    sel = jnp.where(iota((C, 768), 0) == target, 1.0, 0.0).astype(BF16)
    sel_ref[...] = sel
    chi, clo = contacts(state_ref[...], sel)
    chi_ref[...] = chi
    clo_ref[...] = clo
    zev_ref[...], zod_ref[...], y_ref[...] = send_faces(snd, chi, clo, place_ref[1])


def prep_kernel(vol_ref, lift_ref, mass_ref, w_ref, m_ref):
    w_ref[...] = jnp.zeros_like(w_ref)
    high, low = split2(vol_ref[...])
    w_ref[0:C, 0:C] = high
    w_ref[0:C, CP : CP + C] = low
    for face in range(6):
        high, low = split2(lift_ref[face])
        start = CP + 128 * face
        w_ref[start : start + 80, 0:C] = high
        w_ref[start : start + 80, CP : CP + C] = low
    high, low = split2(mass_ref[...])
    m_ref[:, 0:NODES] = high
    m_ref[:, NODES:128] = low


def step_kernel(last, order_ref, place_ref, field_ref, chi_ref, clo_ref, gd_ref, snd_ref, sel_ref, w_ref, m_ref, even_ref, odd_ref, y_ref, *outs):
    rest = list(outs)
    new_ref = rest.pop() if last else rest.pop(0)
    field = field_ref[...]
    fhi, flo = split2(field)
    pad = jnp.zeros((EL, CP - C), BF16)
    his = [fhi, pad]
    los = [flo, pad]
    y_in = y_ref[0:RIM, 0:128]
    even = place_ref[1] == 0
    by_even = even_ref[0:RIM]
    by_odd = odd_ref[...]
    arrived = {2: y_in, 3: y_in, 4: jnp.where(even, by_odd, by_even), 5: jnp.where(even, by_even, by_odd)}
    for face in range(6):
        lanes = slice(128 * face, 128 * face + 128)
        rows = jnp.concatenate([chi_ref[:, lanes], clo_ref[:, lanes]], axis=1)
        if face >= 2:
            ahi, alo = split2(jnp.concatenate([arrived[face], jnp.zeros((8, 128), F32)], axis=0))
            rows = jnp.concatenate([rows, jnp.concatenate([ahi, alo], axis=1)], axis=0)
            picked = mm(gd_ref[face], rows)
        else:
            picked = mm(gd_ref[face, :, 0:EL], rows)
        his.append(picked[:, 0:128].astype(BF16))
        los.append(picked[:, 128:256].astype(BF16))
    both = jnp.concatenate([jnp.concatenate(his, axis=1), jnp.concatenate(los, axis=1)], axis=0)
    prod = mm(both, w_ref[...])
    tend = (prod[:EL, 0:C] + prod[EL:, 0:C]) + (prod[:EL, CP : CP + C] + prod[EL:, CP : CP + C])
    own_block = iota((HALF, 1024), 1) // NODES == iota((HALF, 1024), 0)
    parts = []
    for tile in range(2):
        his = []
        los = []
        for var in range(5):
            one = tend[HALF * tile : HALF * tile + HALF, NODES * var : NODES * var + NODES]
            wide = jnp.concatenate([one, one], axis=1)
            wide = jnp.concatenate([wide] * 8, axis=1)
            high, low = split2(jnp.where(own_block, wide, 0.0))
            his.append(high)
            los.append(low)
        left = jnp.concatenate(his + los, axis=0)
        prod = mm(left, m_ref[1024 * tile : 1024 * tile + 1024, :])
        prod = prod[0:80] + prod[80:160]
        prod = prod[:, 0:NODES] + prod[:, NODES:128]
        parts.append(jnp.concatenate([prod[HALF * var : HALF * var + HALF] for var in range(5)], axis=1))
    new = field + time_step * jnp.concatenate(parts, axis=0)
    new_ref[...] = new
    ana = place_ref[0]
    if last:
        fown_ref, fsend_ref = rest
        first = 0
    else:
        chi_out, clo_out, zev_ref, zod_ref, fsend_ref, fown_ref = rest
        first = RIM
        chi, clo = contacts(new, sel_ref[...])
        chi_out[...] = chi
        clo_out[...] = clo
        zev, zod, y = send_faces(snd_ref[...], chi, clo, place_ref[1])
        zev_ref[...] = zev
        zod_ref[...] = zod
        fsend_ref[0:RIM, 0:128] = y
        fsend_ref[0:RIM, 128:CP] = jnp.zeros((RIM, CP - 128), F32)
    fsend_ref[first : first + HALF, C:CP] = jnp.zeros((HALF, CP - C), F32)
    fown_ref[:, C:CP] = jnp.zeros((HALF, CP - C), F32)
    for k in range(HALF):
        mine = order_ref[0, ana * HALF + k]
        other = order_ref[0, (1 - ana) * HALF + k]
        fown_ref[k : k + 1, 0:C] = new_ref[pl.ds(mine, 1), :]
        fsend_ref[first + k : first + k + 1, 0:C] = new_ref[pl.ds(other, 1), :]


def pick_kernel(order_ref, place_ref, hist_ref, keep_ref, sent_ref, sem):
    ana = place_ref[0]
    copies = []
    for k in range(HALF):
        copies.append(pltpu.make_async_copy(hist_ref.at[order_ref[0, ana * HALF + k]], keep_ref.at[k], sem.at[k]))
        copies.append(
            pltpu.make_async_copy(hist_ref.at[order_ref[0, (1 - ana) * HALF + k]], sent_ref.at[k], sem.at[HALF + k])
        )
    for copy in copies:
        copy.start()
    for copy in copies:
        copy.wait()


def gram_kernel(keep_ref, sent_ref, mine_ref, theirs_ref, full_ref):
    row = iota((64, SNAPS), 0)
    col = iota((64, SNAPS), 1)
    for ref, out_ref in ((keep_ref, mine_ref), (sent_ref, theirs_ref)):
        total = None
        for k in range(0, HALF, 4):
            rows = ref[k : k + 4].reshape(4 * C, HIST)
            part = lax.dot_general(rows, rows, (((0,), (0,)), ((), ())), preferred_element_type=F32)
            total = part if total is None else total + part
        full_ref[...] = jnp.zeros_like(full_ref)
        full_ref[0:HIST, 0:HIST] = total
        last = pltpu.roll(full_ref[64:SNAPS], 64, 1)
        out_ref[0:64] = jnp.where(col < row, last, full_ref[0:64])
        diag = jnp.sum(jnp.where(col == row, last, 0.0), axis=0, keepdims=True)
        out_ref[64:FOLD] = jnp.broadcast_to(diag, (FOLD - 64, SNAPS))


def unfold(folded):
    row = iota((64, SNAPS), 0)
    col = iota((64, SNAPS), 1)
    top = folded[0:64]
    upper = jnp.where(col > row, top, 0.0)
    lower = pltpu.roll(jnp.where(col < row, top, 0.0), 64, 1)
    half = jnp.concatenate([upper, lower], axis=0)
    last = pltpu.roll(jnp.broadcast_to(folded[64:65], (64, SNAPS)), 64, 1)
    diag = jnp.concatenate([jnp.where(col == row, top, 0.0), jnp.where(col == row + 64, last, 0.0)], axis=0)
    return half + half.T + diag


def factor_kernel(scale, gram_ref, up_ref, inv_ref):
    tiles = SNAPS // 8
    row = iota((SNAPS, SNAPS), 0)
    col = iota((SNAPS, SNAPS), 1)
    start = jnp.where((row < HIST) & (col < HIST), unfold(gram_ref[...]) * scale, jnp.where(row == col, 1.0, 0.0))
    ident = jnp.where(row == col, 1.0, 0.0)
    on = jnp.where(row == col, start, 0.0)
    across = jnp.sum(on, axis=0, keepdims=True)
    shrink = 1.0 / jnp.sqrt(across)
    start = start * (1.0 / jnp.sqrt(jnp.sum(on, axis=1, keepdims=True))) * shrink
    a = [start[8 * t : 8 * t + 8] for t in range(tiles)]
    b = [ident[8 * t : 8 * t + 8] for t in range(tiles)]
    below = iota((8, SNAPS), 0)
    full = (8, SNAPS)
    for j in range(0, HIST, 2):
        t = j // 8
        r = j % 8
        m0 = {k: jnp.broadcast_to(a[k][:, j : j + 1], full) for k in range(t, tiles)}
        m1 = {k: jnp.broadcast_to(a[k][:, j + 1 : j + 2], full) for k in range(t, tiles)}
        p = jnp.broadcast_to(m0[t][r : r + 1], full)
        q = jnp.broadcast_to(m0[t][r + 1 : r + 2], full)
        s = jnp.broadcast_to(m1[t][r + 1 : r + 2], full)
        a0 = jnp.broadcast_to(a[t][r : r + 1], full)
        a1 = jnp.broadcast_to(a[t][r + 1 : r + 2], full)
        b0 = jnp.broadcast_to(b[t][r : r + 1], full)
        b1 = jnp.broadcast_to(b[t][r + 1 : r + 2], full)
        inv = 1.0 / (p * s - q * q)
        ip = s * inv
        iq = q * inv
        js = p * inv
        sa0 = ip * a0 - iq * a1
        sa1 = js * a1 - iq * a0
        sb0 = ip * b0 - iq * b1
        sb1 = js * b1 - iq * b0
        for k in range(t, tiles):
            if k == t:
                if r == 6:
                    continue
                m0[k] = jnp.where(below > r + 1, m0[k], 0.0)
                m1[k] = jnp.where(below > r + 1, m1[k], 0.0)
            a[k] = a[k] - m0[k] * sa0 - m1[k] * sa1
            b[k] = b[k] - m0[k] * sb0 - m1[k] * sb1
    up = jnp.concatenate(a, axis=0)
    low = jnp.concatenate(b, axis=0)
    odd = (iota((SNAPS, 1), 0) % 2) == 1
    diag = jnp.sum(jnp.where(row == col, up, 0.0), axis=1, keepdims=True)
    side = jnp.sum(jnp.where(row == col + 1, up, 0.0), axis=1, keepdims=True)
    before = pltpu.roll(jnp.broadcast_to(diag, (SNAPS, SNAPS)), 1, 0)[:, 0:1]
    ratio = jnp.where(odd, side / before, 0.0)
    root = 1.0 / jnp.sqrt(diag - ratio * side)
    up = (up - ratio * pltpu.roll(up, 1, 0)) * root
    low = (low - ratio * pltpu.roll(low, 1, 0)) * root
    up_ref[...] = jnp.where(col >= row, up, 0.0) * (across * shrink)
    inv_ref[...] = jnp.where(col <= row, low, 0.0) * shrink


def rows_kernel(fields_ref, keep_ref, other_ref, out_ref, turned_ref):
    f = fields_ref[...]
    high = f.astype(BF16).astype(F32)
    mid = (f - high).astype(BF16).astype(F32)
    low = f - high - mid
    zero = jnp.zeros((4, C), F32)
    total = None
    for half, ref in ((0, keep_ref), (1, other_ref)):
        for k in range(HALF):
            at = slice(64 * half + 4 * k, 64 * half + 4 * k + 4)
            left = jnp.concatenate([high[at, 0:C], mid[at, 0:C], low[at, 0:C], zero], axis=0).astype(BF16)
            part = mm(left, ref[k])
            total = part if total is None else total + part
    rows = total[0:4] + total[4:8] + total[8:12]
    rows = jnp.concatenate([rows, jnp.zeros((4, 4), F32)], axis=1)
    lane = iota((4, SNAPS), 1)
    sub = iota((4, SNAPS), 0)
    for d in range(STEPS):
        other = f if d == 0 else pltpu.roll(f, SNAPS - d, 0)
        pair = jnp.sum(f * other, axis=1, keepdims=True)
        for s in range(STEPS - d):
            both = jnp.sum(jnp.where(iota((SNAPS, 1), 0) % 4 == s, pair, 0.0), axis=0, keepdims=True)
            at = (sub == s) & (lane == HIST + s + d)
            at = at | ((sub == s + d) & (lane == HIST + s))
            rows = jnp.where(at, both, rows)
    out_ref[...] = jnp.broadcast_to(rows[None], out_ref.shape)
    turned = f.T[0:C]
    high, low = split2(turned)
    turned_ref[:, 0:SNAPS] = high
    turned_ref[:, SNAPS : 2 * SNAPS] = low


def border_kernel(scale, gathered_ref, up_ref, inv_ref, w_ref, wf_ref, fac_ref):
    rows = jnp.sum(gathered_ref[...], axis=0) * scale
    lane = iota((4, SNAPS), 1)
    g21 = jnp.where(lane < HIST, rows, 0.0)
    inv = inv_ref[...]
    l21 = lax.dot_general(g21, inv, (((1,), (1,)), ((), ())), precision=HIGHEST, preferred_element_type=F32)
    l21 = jnp.where(lane < HIST, l21, 0.0)
    comp = [[None] * 4 for _ in range(4)]
    for s in range(4):
        for u in range(s, 4):
            g = jnp.sum(jnp.where(lane[0:1] == HIST + u, rows[s : s + 1], 0.0), axis=1, keepdims=True)
            comp[s][u] = g - jnp.sum(l21[s : s + 1] * l21[u : u + 1], axis=1, keepdims=True)
    tail = lax.dot_general(l21, inv, (((1,), (0,)), ((), ())), precision=HIGHEST, preferred_element_type=F32)
    unit = jnp.where(lane == iota((4, SNAPS), 0) + HIST, 1.0, 0.0)
    work = [unit[s : s + 1] - tail[s : s + 1] for s in range(4)]
    ups = []
    outs = []
    for s in range(4):
        root = 1.0 / jnp.sqrt(comp[s][s])
        urow = [None] * 4
        for u in range(s, 4):
            urow[u] = comp[s][u] * root
        ups.append(urow)
        outs.append(work[s] * root)
        for u in range(s + 1, 4):
            work[u] = work[u] - urow[u] * outs[s]
            for v in range(u, 4):
                comp[u][v] = comp[u][v] - urow[u] * urow[v]
    new_rows = jnp.concatenate(outs, axis=0)
    full = jnp.concatenate([inv[0:HIST], new_rows], axis=0)
    wide = full.T
    high, low = split2(wide)
    w_ref[:, 0:SNAPS] = high
    w_ref[:, SNAPS : 2 * SNAPS] = low
    ends = jnp.concatenate([high[HIST:], low[HIST:]], axis=1).astype(F32)
    ends = jnp.concatenate([ends, ends], axis=0)
    wf_ref[...] = jnp.concatenate([ends] * 32, axis=0).astype(BF16)
    tri = jnp.zeros((4, SNAPS), F32)
    sub = iota((4, SNAPS), 0)
    for s in range(4):
        for u in range(s, 4):
            tri = jnp.where((sub == s) & (lane == HIST + u), ups[s][u], tri)
    lower = up_ref[...].T
    lower = jnp.concatenate([lower[0:HIST], l21], axis=0)
    upper = lower.T
    fac_ref[0] = jnp.concatenate([upper[0:HIST], tri], axis=0)


def final_kernel(place_ref, w_ref, wf_ref, turned_ref, keep_ref, other_ref, out_ref, buf_ref, sem):
    ana = place_ref[0]
    main = w_ref[0:HIST, :]
    ends = wf_ref[...]
    turned = turned_ref[...]
    element = (iota((1, 2 * SNAPS), 1) % SNAPS) // 4
    copies = []
    for at in range(0, HALF, FINAL):
        for half, which, ref in ((0, ana, keep_ref), (1, 1 - ana, other_ref)):
            own = [
                turned * jnp.where(element == at + k + HALF * half, 1.0, 0.0).astype(BF16) for k in range(FINAL)
            ]
            rows = ref[at : at + FINAL].reshape(FINAL * C, HIST)
            prod = mm(rows, main) + mm(jnp.concatenate(own, axis=0), ends)
            prod = (prod[:, 0:SNAPS] + prod[:, SNAPS : 2 * SNAPS]).reshape(FINAL, C, SNAPS)
            buf_ref[half, at : at + FINAL] = prod
            copy = pltpu.make_async_copy(
                buf_ref.at[half, pl.ds(at, FINAL)],
                out_ref.at[which, pl.ds(at, FINAL)],
                sem.at[len(copies)],
            )
            copy.start()
            copies.append(copy)
    for copy in copies:
        copy.wait()


def shape(dims, kind=F32):
    return jax.ShapeDtypeStruct(dims, kind)


SMEM = pl.BlockSpec(memory_space=pltpu.SMEM)
VMEM = pl.BlockSpec(memory_space=pltpu.VMEM)
ANY = pl.BlockSpec(memory_space=pltpu.HBM)
PARAMS = pltpu.CompilerParams(vmem_limit_bytes=40 << 20)


def in_hbm(x):
    return pltpu.with_memory_space_constraint(x, pltpu.HBM)


def body(state, history, inv_mass, vol_op, lift_ops, neighbors, owner):
    groups = lax.axis_size("solver")
    place = jnp.stack([lax.axis_index("ana"), lax.axis_index("solver") % 2]).astype(I32)
    base = (lax.axis_index(("solver", "ana")) * EL).astype(I32).reshape(1)
    hist = in_hbm(jnp.transpose(history, (1, 2, 0)))
    mass = jnp.transpose(inv_mass, (2, 0, 1)).reshape(EL * NODES, NODES)
    scale = 1.0 / (EL * C * groups)
    evens = [(i, i ^ 1) for i in range(groups)]
    odds = [(i, (i + 1 if i % 2 else i - 1) % groups) for i in range(groups)]
    swap = [(0, 1), (1, 0)]

    gd, snd, order, sel, chi, clo, zev, zod, yout = pl.pallas_call(
        setup_kernel,
        in_specs=[SMEM, SMEM, ANY, ANY, ANY],
        scratch_shapes=[
            pltpu.VMEM((6, EL), I32),
            pltpu.VMEM((1, EL), I32),
            pltpu.VMEM((EL, C), F32),
            pltpu.SemaphoreType.DMA((3,)),
        ],
        out_shape=(
            shape((6, EL, 48), BF16),
            shape((EL, EL), BF16),
            shape((1, EL), I32),
            shape((C, 768), BF16),
            shape((EL, 768), BF16),
            shape((EL, 768), BF16),
            shape((RIM, 128)),
            shape((RIM, 128)),
            shape((RIM, 128)),
        ),
        compiler_params=PARAMS,
        name="setup",
    )(base, place, in_hbm(neighbors), in_hbm(owner.reshape(1, EL)), in_hbm(state))

    keep, sent = pl.pallas_call(
        pick_kernel,
        in_specs=[SMEM, SMEM, ANY],
        out_shape=(shape((HALF, C, HIST), BF16), shape((HALF, C, HIST), BF16)),
        scratch_shapes=[pltpu.SemaphoreType.DMA((2 * HALF,))],
        compiler_params=PARAMS,
        name="pick",
    )(order, place, hist)
    w, m = pl.pallas_call(
        prep_kernel,
        in_specs=[VMEM, VMEM, VMEM],
        out_shape=(shape((CP + 768, 2 * CP), BF16), shape((EL * NODES, 128), BF16)),
        compiler_params=PARAMS,
        name="prep",
    )(vol_op, lift_ops, mass)

    gram, theirs = pl.pallas_call(
        gram_kernel,
        in_specs=[VMEM, VMEM],
        out_shape=(shape((FOLD, SNAPS)), shape((FOLD, SNAPS))),
        scratch_shapes=[pltpu.VMEM((SNAPS, SNAPS), F32)],
        compiler_params=PARAMS,
        name="gram",
    )(keep, sent)
    field = state
    owns = []
    recvs = []
    bits = [1 << k for k in range(groups.bit_length() - 1)]
    stages = [[], bits[1:3], bits[3:5], bits[5:7], bits[0:1]]

    def summed(gram, two):
        total = gram
        if not two:
            return gram
        for bit in two + ([two[0] | two[1]] if len(two) == 2 else []):
            total = total + lax.ppermute(gram, "solver", [(i, i ^ bit) for i in range(groups)])
        return total

    for step in range(STEPS):
        even = lax.ppermute(zev, "solver", evens)
        gram = summed(gram, stages[step])
        odd = lax.ppermute(zod, "solver", odds)
        yin = lax.ppermute(yout, "ana", swap)
        if step == 0:
            theirs, sent, even, odd, yin = lax.optimization_barrier((theirs, sent, even, odd, yin))
            gram = gram + lax.ppermute(theirs, "ana", swap)
            other = lax.ppermute(sent, "ana", swap)
        else:
            even, odd, yin, gram, other = lax.optimization_barrier((even, odd, yin, gram, other))
        if step:
            recvs.append(yin[RIM:])
        last = step == STEPS - 1
        outs = [shape((HALF, CP))]
        if last:
            outs = outs + [shape((HALF, CP)), shape((EL, C))]
        else:
            outs = [
                shape((EL, C)),
                shape((EL, 768), BF16),
                shape((EL, 768), BF16),
                shape((RIM, 128)),
                shape((RIM, 128)),
                shape((RIM + HALF, CP)),
            ] + outs
        res = pl.pallas_call(
            functools.partial(step_kernel, last),
            in_specs=[SMEM, SMEM] + [VMEM] * 11,
            out_shape=tuple(outs),
            compiler_params=PARAMS,
            name="step",
        )(order, place, field, chi, clo, gd, snd, sel, w, m, even, odd, yin)
        if last:
            own, rows_out = res[0], res[1]
        else:
            field, chi, clo, zev, zod, yout, own = res
            gram, zev, zod, yout = lax.optimization_barrier((gram, zev, zod, yout))
        owns.append(own)
    recvs.append(lax.ppermute(rows_out, "ana", swap))
    fields = jnp.stack([jnp.stack(owns, axis=1), jnp.stack(recvs, axis=1)]).reshape(SNAPS, CP)

    gram = summed(gram, stages[STEPS])
    up, inv = pl.pallas_call(
        functools.partial(factor_kernel, scale),
        in_specs=[VMEM],
        out_shape=(shape((SNAPS, SNAPS)), shape((SNAPS, SNAPS))),
        compiler_params=PARAMS,
        name="factor",
    )(gram)

    rows, turned = pl.pallas_call(
        rows_kernel,
        in_specs=[VMEM, VMEM, VMEM],
        out_shape=(shape((groups, STEPS, SNAPS)), shape((C, 2 * SNAPS), BF16)),
        compiler_params=PARAMS,
        name="rows",
    )(fields, keep, other)
    gathered = lax.all_to_all(rows, "solver", 0, 0, tiled=True)

    wide, wf, fac = pl.pallas_call(
        functools.partial(border_kernel, scale),
        in_specs=[VMEM, VMEM, VMEM],
        out_shape=(shape((SNAPS, 2 * SNAPS), BF16), shape((2 * SNAPS, 2 * SNAPS), BF16), shape((1, SNAPS, SNAPS))),
        compiler_params=PARAMS,
        name="border",
    )(gathered, up, inv)

    coef = pl.pallas_call(
        final_kernel,
        in_specs=[SMEM] + [VMEM] * 5,
        out_specs=ANY,
        out_shape=shape((2, HALF, C, SNAPS)),
        scratch_shapes=[
            pltpu.VMEM((2, HALF, C, SNAPS), F32),
            pltpu.SemaphoreType.DMA((2 * HALF // FINAL,)),
        ],
        compiler_params=PARAMS,
        name="final",
    )(place, wide, wf, turned, keep, other)
    return coef.reshape(EL, C, SNAPS), fac


def solution(mesh):
    return jax.shard_map(
        body,
        mesh=mesh,
        in_specs=(
            P(("solver", "ana"), None),
            P(None, ("solver", "ana"), None),
            P(None, None, ("solver", "ana")),
            P(),
            P(),
            P(None, ("solver", "ana")),
            P(("solver", "ana")),
        ),
        out_specs=(P(("solver", "ana"), None, None), P("ana", None, None)),
        check_vma=False,
    )
```
